128 devices in a mesh: ctx: 16 (over z, y_hi, core), kvh: 8 (over x, y_lo).
Axes of the slice: x: 4, y: 4 (y_hi: 2, y_lo: 2; y = y_hi * 2 + y_lo), z: 4, core: 2. Of those that a mesh axis runs over, the one named last changes fastest.
Arguments:
- query_rows: bfloat16 [16384, 2048], P('ctx', 'kvh'), may hold values from -10 to 10
- key_rows: bfloat16 [16384, 512], P('ctx', 'kvh'), may hold values from -6 to 6
- value_rows: bfloat16 [16384, 512], P('ctx', 'kvh'), may hold values from -6 to 6
- out_weight: bfloat16 [2048, 2880], P('kvh'), may hold values from -6 to 6
- residual: bfloat16 [16384, 2880], P(('ctx', 'kvh')), may hold values from -6 to 6
- norm_gain: float32 [2880], replicated, may hold values from 0.1 to 1.9
- gate_weight: bfloat16 [2880, 92160], P(None, ('ctx', 'kvh')), may hold values from -0.109375 to 0.109375
- up_weight: bfloat16 [2880, 92160], P(None, ('ctx', 'kvh')), may hold values from -0.109375 to 0.109375
- down_weight: bfloat16 [92160, 2880], P(('ctx', 'kvh')), may hold values from -0.15625 to 0.15625
- expert_ids: int32 [16384, 4], P(('ctx', 'kvh')), may hold values from 0 to 63, all different within a row; in each aligned block of 128 rows (0 to 127, 128 to 255, ...) at most 10 rows name the same one
- route_weights: float32 [16384, 4], P(('ctx', 'kvh')), may hold values from 0.05 to 1
Outputs:
- layer_out: bfloat16 [16384, 2880], P(('ctx', 'kvh'))
The draws below stay inside these ranges and needn't reach their ends.
Inputs may be any that keep to these rules, and one draw needn't show every extreme that they name: `expert_ids`: each row names 4 different experts. Within the rows of one device (aligned blocks of 128 rows) no expert is named by more than 10 rows, and in every draw some expert in some block is named by exactly 10 rows.
All inputs are finite; a program needn't handle non-finite values.
Results may differ from the reference program's by a relative error of at most 0.02.
Values may be sent and summed in bfloat16 or wider, within the bound.
A program may use at most 192 MiB of HBM per device.

```python
import math
import jax
import jax.numpy as jnp
import numpy as np
from jax import lax

D = 2880
HEAD = 64
KVH = 8
HEADS = 32
FFW = 1440
TOP = 4
TOK_DEV = 128
SEQ = 16384
EXPERTS = 64
CAP = 10
N_CTX = 16
N_KVH = 8


def draw_query_rows(key, part):
    own_key = jax.random.fold_in(key, 1)
    values = jnp.clip(jax.random.normal(own_key, (SEQ, HEADS * HEAD), jnp.float32), -6.0, 6.0)
    return values.astype(jnp.bfloat16)


def draw_key_rows(key, part):
    own_key = jax.random.fold_in(key, 2)
    values = jnp.clip(jax.random.normal(own_key, (SEQ, KVH * HEAD), jnp.float32), -6.0, 6.0)
    return values.astype(jnp.bfloat16)


def level_of(key, extent, shards, smallest, largest):
    level, own = 1.0, jax.random.fold_in(key, 6)
    for axis_at, shards_of in shards:
        steps = jnp.exp(jax.random.uniform(jax.random.fold_in(own, axis_at), (shards_of,), jnp.float32, smallest / len(shards), largest / len(shards)))
        level = level * jnp.repeat(steps, extent[axis_at] // shards_of).reshape([-1 if axis == axis_at else 1 for axis in range(len(extent))])
    return level


def assign_block(key, own, number, rows, amount, top, limit, skew):
    order = jax.random.permutation(key, amount)
    crowded, ordinary = load_shares(amount, rows * top, limit, skew, True), load_shares(amount, rows * top, limit, skew, False)
    places = jnp.arange(amount)

    def named(tallies, offset_by):
        used = int((tallies > 0).sum())
        fixed = max(1, used // 4)
        shifted = fixed + (places - fixed + offset_by * (used - fixed)) % max(1, amount - fixed)
        return jnp.zeros((amount,), jnp.int32).at[order[jnp.where(places < fixed, places, shifted)]].set(jnp.asarray(tallies, jnp.int32))

    tallies = jnp.where(number % 4 == 0, named(crowded, number // 4), named(ordinary, number - number // 4 - 1))
    mixed = jax.random.permutation(jax.random.fold_in(own, 3), amount)
    giver, sink = mixed[0:amount // 2 * 2:2], mixed[1:amount // 2 * 2:2]
    slack = jnp.minimum(tallies[giver] - 1, limit - tallies[sink]) // 2
    slack = jnp.where((giver == order[0]) | (sink == order[0]) | (tallies[sink] == 0), 0, jnp.maximum(slack, 0))
    shifted = jax.random.randint(jax.random.fold_in(own, 4), (amount // 2,), 0, 1 << 20) % (slack + 1)
    tallies = tallies.at[giver].add(-shifted).at[sink].add(shifted)
    members = jnp.searchsorted(jnp.cumsum(tallies), jnp.arange(rows * top), side="right").astype(jnp.int32)
    listing = members.reshape(top, rows).T
    listing = listing[jax.random.permutation(jax.random.fold_in(own, 1), rows)]
    offset_by = jax.random.randint(jax.random.fold_in(own, 2), (rows, 1), 0, top)
    return jnp.take_along_axis(listing, (jnp.arange(top)[None, :] + offset_by) % top, axis=1)


def load_shares(count, total, reach, lean, full):
    loads = [(1 << 20) // math.isqrt(standing ** lean) + 1 for standing in range(1, count + 1)]
    largest = reach if full else min(reach, max(-(-total // count), total * loads[0] // sum(loads)))
    least = 1 if total - largest >= count - 1 else 0
    given, rest = [largest] + [least] * (count - 1), total - largest - least * (count - 1)
    while rest > 0:
        candidates = [i for i in range(1, count) if given[i] < largest] or [i for i in range(1, count) if given[i] < reach]
        mass, left = sum([loads[i] for i in candidates]), rest
        for i in candidates:
            more = min(reach - given[i], max(1, left * loads[i] // mass), rest)
            given[i] = given[i] + more
            rest = rest - more
    return np.array(given)


def gaussian(stream_key, extent, scale, most, cuts=(), held_as=jnp.bfloat16):
    values = scale * jax.random.normal(stream_key, extent, jnp.float32)
    if cuts:
        values = values * level_of(stream_key, extent, cuts, -0.22, 0.18)
    return jnp.clip(values, -most, most).astype(held_as)


def setup_inputs(seed: int = 0) -> dict:
    seeds = jax.random.split(jax.random.key(seed), 12)
    query_rows = draw_query_rows(jax.random.fold_in(seeds[11], 71), 0)
    key_rows = draw_key_rows(jax.random.fold_in(seeds[11], 71), 0)
    value_rows = gaussian(seeds[2], (SEQ, KVH * HEAD), 1.0, 6.0, ((0, 16), (1, 8)))
    out_weight = gaussian(seeds[3], (HEADS * HEAD, D), 1.0, 6.0, ((0, 8),))
    residual = gaussian(seeds[4], (SEQ, D), 1.0, 6.0, ((0, 128),))
    norm_gain = jnp.clip(1.0 + 0.18 * jax.random.normal(seeds[5], (D,), jnp.float32), 0.1, 1.9)
    gate_weight = gaussian(seeds[6], (D, EXPERTS * FFW), D ** -0.5, 0.109375, ((1, 128),))
    up_weight = gaussian(seeds[7], (D, EXPERTS * FFW), D ** -0.5, 0.109375, ((1, 128),))
    down_weight = gaussian(seeds[8], (EXPERTS * FFW, D), FFW ** -0.5, 0.15625, ((0, 128),))
    expert_ids_keys = jax.random.split(jax.random.fold_in(seeds[9], 1), SEQ // TOK_DEV)
    expert_ids_turns = jax.random.permutation(jax.random.fold_in(seeds[9], 3), SEQ // TOK_DEV)
    expert_ids = jax.vmap(lambda own, number: assign_block(jax.random.fold_in(seeds[9], 2), own, number, TOK_DEV, EXPERTS, TOP, CAP, 2))(expert_ids_keys, expert_ids_turns).reshape((SEQ, TOP))
    route_weights = jnp.clip(0.05 + 0.95 * jax.random.uniform(seeds[10], (SEQ, TOP), jnp.float32) ** level_of(seeds[10], (SEQ, TOP), ((0, 128),), -0.2, 0.2), 0.05, 1.0)
    return {"query_rows": query_rows, "key_rows": key_rows, "value_rows": value_rows, "out_weight": out_weight, "residual": residual, "norm_gain": norm_gain, "gate_weight": gate_weight, "up_weight": up_weight, "down_weight": down_weight, "expert_ids": expert_ids, "route_weights": route_weights}


def attend_heads(query_rows, key_rows, value_rows):
    group = HEADS // KVH
    block = min(512, SEQ)
    key_pos = jnp.arange(SEQ, dtype=jnp.int32)
    firsts = jnp.arange(SEQ // block, dtype=jnp.int32) * block
    columns = []
    for kv_index in range(KVH):
        keys_f = key_rows[:, kv_index * HEAD:(kv_index + 1) * HEAD].astype(jnp.float32)
        vals_f = value_rows[:, kv_index * HEAD:(kv_index + 1) * HEAD].astype(jnp.float32)
        queries_h = query_rows[:, kv_index * group * HEAD:(kv_index + 1) * group * HEAD]
        queries_h = queries_h.reshape(SEQ // block, block, group, HEAD)

        def one_block(pair):
            q_block, first = pair
            q_pos = first + jnp.arange(block, dtype=jnp.int32)
            allowed = q_pos[:, None] >= key_pos[None, :]
            scores = jnp.einsum('qgd,kd->gqk', q_block.astype(jnp.float32), keys_f) * HEAD ** (-0.5)
            scores = jnp.where(allowed[None], scores, -1e+30)
            top_score = lax.optimization_barrier(jnp.max(scores, axis=-1, keepdims=True))
            probs = jnp.where(allowed[None], jnp.exp(scores - top_score), 0.0)
            total = lax.optimization_barrier(jnp.sum(probs, axis=-1))
            rounded = lax.optimization_barrier(probs.astype(jnp.bfloat16)).astype(jnp.float32)
            result = jnp.einsum('gqk,kd->gqd', rounded, vals_f) / total[..., None]
            return result.transpose(1, 0, 2).astype(jnp.bfloat16)
        blocks_out = lax.map(one_block, (queries_h, firsts))
        columns.append(blocks_out.reshape(SEQ, group * HEAD))
    return jnp.concatenate(columns, axis=1)

def expert_ffn(rows, gate_cols, up_cols, down_rows):
    gate_part = jnp.dot(rows, gate_cols, preferred_element_type=jnp.float32)
    up_part = jnp.dot(rows, up_cols, preferred_element_type=jnp.float32)
    act = ((up_part + 1.0) * gate_part * jax.nn.sigmoid(1.702 * gate_part)).astype(jnp.bfloat16)
    return jnp.dot(act, down_rows, preferred_element_type=jnp.float32)

def reference(query_rows, key_rows, value_rows, out_weight, residual, norm_gain, gate_weight, up_weight, down_weight, expert_ids, route_weights):
    attended = attend_heads(query_rows, key_rows, value_rows)
    width = HEADS * HEAD // N_KVH
    projected = jnp.zeros((SEQ, D), jnp.float32)
    for group_index in range(N_KVH):
        part = jnp.dot(attended[:, group_index * width:(group_index + 1) * width], out_weight[group_index * width:(group_index + 1) * width], preferred_element_type=jnp.float32)
        projected = projected + lax.optimization_barrier(part.astype(jnp.bfloat16)).astype(jnp.float32)
    hidden = residual.astype(jnp.float32) + projected
    normed = (hidden * lax.rsqrt(lax.optimization_barrier(jnp.mean(hidden * hidden, axis=-1, keepdims=True)) + 1e-05) * norm_gain).astype(jnp.bfloat16)
    flat_ids = expert_ids.reshape(-1).astype(jnp.int32)
    flat_weights = route_weights.reshape(-1)
    order = jnp.argsort(flat_ids, stable=True).astype(jnp.int32)
    counts = lax.optimization_barrier(jnp.sum((flat_ids[:, None] == jnp.arange(EXPERTS, dtype=jnp.int32)[None, :]).astype(jnp.int32), axis=0))
    offsets = jnp.cumsum(counts) - counts
    most_rows = N_CTX * N_KVH * CAP
    last_index = SEQ * TOP - 1

    def one_expert(total, expert):
        index_run = offsets[expert] + jnp.arange(most_rows, dtype=jnp.int32)
        valid = jnp.arange(most_rows, dtype=jnp.int32) < counts[expert]
        picked = order[jnp.clip(index_run, 0, last_index)]
        tokens = (picked // TOP).astype(jnp.int32)
        rows = normed[tokens]
        start = (expert * FFW).astype(jnp.int32)
        gate_cols = lax.dynamic_slice_in_dim(gate_weight, start, FFW, 1)
        up_cols = lax.dynamic_slice_in_dim(up_weight, start, FFW, 1)
        down_rows = lax.dynamic_slice_in_dim(down_weight, start, FFW, 0)
        result = expert_ffn(rows, gate_cols, up_cols, down_rows)
        scale = jnp.where(valid, flat_weights[picked], 0.0)
        return (total.at[tokens].add(result * scale[:, None]), None)
    moe, _ = lax.scan(one_expert, jnp.zeros((SEQ, D), jnp.float32), jnp.arange(EXPERTS, dtype=jnp.int32))
    return (hidden + moe).astype(jnp.bfloat16)
```

```python
import jax
import jax.numpy as jnp
from jax import lax
from jax.experimental import pallas as pl
from jax.experimental.pallas import tpu as pltpu
from jax.sharding import PartitionSpec as P

HEAD = 64
GROUP = 4
TOP = 4
BLK = 512
KEYS = 1024
LOW = -1e30
LOG2E = 1.4426950408889634


def flash_kernel(ctx_size, q_ref, kv_ref, o_ref, qs, m_ref, acc):
    me = lax.axis_index("ctx")
    last = 2 * ctx_size - 1
    even = lax.rem(me, 2) == 0
    numbers = (jnp.where(even, me, last - me), jnp.where(even, last - me, me))
    qs[...] = jnp.zeros_like(qs)
    ones = jnp.ones((KEYS, 128), jnp.bfloat16)
    for s in range(2):
        number = numbers[s]
        for h in range(GROUP):
            q = q_ref[s, :, h * HEAD : (h + 1) * HEAD].astype(jnp.float32) * (0.125 * LOG2E)
            hi = q.astype(jnp.bfloat16)
            lo = (q - hi.astype(jnp.float32)).astype(jnp.bfloat16)
            qs[h, :, 0:HEAD] = hi
            qs[h, :, 128 : 128 + HEAD] = lo
        m_ref[...] = jnp.full_like(m_ref, LOW)
        acc[...] = jnp.zeros_like(acc)

        def fold(start, masked, number=number):
            kv = kv_ref[pl.ds(pl.multiple_of(start, BLK), KEYS), :]
            rhs_k = jnp.concatenate([kv, kv], axis=1)
            rhs_v = jnp.concatenate([kv, ones], axis=1)
            if masked:
                row = number * BLK + lax.broadcasted_iota(jnp.int32, (BLK, KEYS), 0)
                col = start + lax.broadcasted_iota(jnp.int32, (BLK, KEYS), 1)
                allowed = row >= col
            for h in range(GROUP):
                sc = lax.dot_general(
                    qs[h], rhs_k, (((1,), (1,)), ((), ())), preferred_element_type=jnp.float32
                )
                if masked:
                    sc = jnp.where(allowed, sc, LOW)
                m_old = m_ref[h]
                m_new = jnp.maximum(m_old, jnp.max(sc, axis=1, keepdims=True))
                alpha = jnp.exp2(m_old - m_new)
                p = jnp.exp2(sc - m_new[:, :1]).astype(jnp.bfloat16)
                pv = jnp.dot(p, rhs_v, preferred_element_type=jnp.float32)
                acc[h] = acc[h] * jnp.concatenate([alpha, alpha], axis=1) + pv
                m_ref[h] = m_new

        half = number // 2

        def body(j, carry, fold=fold):
            fold(j * KEYS, False)
            return carry

        lax.fori_loop(0, half, body, 0)
        fold(half * KEYS, True)
        parts = []
        for h in range(GROUP):
            a = acc[h]
            parts.append(a[:, HEAD : 2 * HEAD] / a[:, 128 : 128 + HEAD])
        o_ref[s] = jnp.concatenate(parts, axis=1).astype(jnp.bfloat16)


def flash(q2, kv_all, ctx_size):
    return pl.pallas_call(
        lambda *refs: flash_kernel(ctx_size, *refs),
        out_shape=jax.ShapeDtypeStruct(q2.shape, jnp.bfloat16),
        in_specs=[pl.BlockSpec(memory_space=pltpu.VMEM)] * 2,
        out_specs=pl.BlockSpec(memory_space=pltpu.VMEM),
        scratch_shapes=[
            pltpu.VMEM((GROUP, BLK, 256), jnp.bfloat16),
            pltpu.VMEM((GROUP, BLK, 128), jnp.float32),
            pltpu.VMEM((GROUP, BLK, 256), jnp.float32),
        ],
        compiler_params=pltpu.CompilerParams(vmem_limit_bytes=48 << 20),
        cost_estimate=pl.CostEstimate(
            flops=80_000_000_000, bytes_accessed=6_000_000, transcendentals=40_000_000
        ),
        name="flash",
    )(q2, kv_all)


def shards(
    query_rows,
    key_rows,
    value_rows,
    out_weight,
    residual,
    norm_gain,
    gate_weight,
    up_weight,
    down_weight,
    expert_ids,
    route_weights,
):
    nc, nk = lax.axis_size("ctx"), lax.axis_size("kvh")
    both = ("ctx", "kvh")
    rows = query_rows.shape[0]
    token_count, width = residual.shape

    swap, cross = [], []
    for zy in range(nc // 2):
        for core in range(2):
            for x in range(nk // 2):
                for y in range(2):
                    here = (zy * 2 + core) * nk + x * 2 + y
                    there = (zy * 2 + y) * nk + x * 2 + core
                    swap.append((here, there))
                    cross.append((here, (zy * 2 + 1 - core) * nk + x * 2 + y))
    mine = [lax.ppermute(w, both, swap) for w in (gate_weight, up_weight, down_weight)]
    other = [lax.ppermute(w, both, cross) for w in mine]

    kv_all = lax.all_gather(jnp.concatenate([key_rows, value_rows], axis=1), "ctx", axis=0, tiled=True)
    even = [(j, 2 * j if 2 * j < nc else 2 * nc - 1 - 2 * j) for j in range(nc)]
    odd = [(j, 2 * j + 1 if 2 * j + 1 < nc else 2 * nc - 2 - 2 * j) for j in range(nc)]
    q_even = lax.ppermute(query_rows[: rows // 2], "ctx", even)
    q_odd = lax.ppermute(query_rows[rows // 2 :], "ctx", odd)
    attended2 = flash(jnp.stack([q_even, q_odd]), kv_all, nc)
    a_even = lax.ppermute(attended2[0], "ctx", [(b, a) for a, b in even])
    a_odd = lax.ppermute(attended2[1], "ctx", [(b, a) for a, b in odd])
    attended = jnp.concatenate([a_even, a_odd], axis=0)
    weight_all = lax.all_gather(out_weight, "kvh", axis=0, tiled=True)
    heads = lax.all_to_all(attended, "kvh", split_axis=0, concat_axis=1, tiled=True)
    projected = jnp.dot(heads, weight_all, preferred_element_type=jnp.float32)
    hidden = residual.astype(jnp.float32) + projected
    normed = (
        hidden * lax.rsqrt(jnp.mean(hidden * hidden, axis=-1, keepdims=True) + 1e-05) * norm_gain
    ).astype(jnp.bfloat16)

    device_count = nc * nk
    expert_count = device_count // 2
    capacity = 2 * max(1, 5 * token_count * TOP // (8 * expert_count))
    half_cap = capacity // 2
    slots_total = expert_count * capacity
    flat_ids = expert_ids.reshape(-1)
    onehot = (flat_ids[:, None] == jnp.arange(expert_count, dtype=jnp.int32)[None, :]).astype(
        jnp.int32
    )
    before = jnp.cumsum(onehot, axis=0) - onehot
    slot = jnp.sum(before * onehot, axis=1)
    per_zy = nk
    zy, c, x = flat_ids // per_zy, (flat_ids // (nk // 2)) % 2, flat_ids % (nk // 2)
    dest = (zy * 2 + slot // half_cap) * nk + x * 2 + c
    target = (dest * half_cap + slot % half_cap).reshape(token_count, TOP)
    slot_iota = jnp.arange(slots_total, dtype=jnp.int32)
    matches = slot_iota[None, None, :] == target[:, :, None]
    placing = jnp.any(matches, axis=1).astype(jnp.bfloat16)
    mixing = jnp.sum(jnp.where(matches, route_weights[:, :, None], 0.0), axis=1)
    outgoing = jnp.einsum("ts,td->sd", placing, normed, preferred_element_type=jnp.float32).astype(
        jnp.bfloat16
    )
    outgoing = outgoing.reshape(device_count, half_cap, width)
    items = lax.all_to_all(outgoing, both, split_axis=0, concat_axis=0, tiled=True)
    flat = items.reshape(slots_total, width)

    def half_expert(gate_w, up_w, down_w):
        gate = jnp.dot(flat, gate_w, preferred_element_type=jnp.float32)
        up = jnp.dot(flat, up_w, preferred_element_type=jnp.float32)
        act = ((up + 1.0) * gate * jax.nn.sigmoid(1.702 * gate)).astype(jnp.bfloat16)
        return jnp.dot(act, down_w, preferred_element_type=jnp.float32)

    result = (half_expert(*mine) + half_expert(*other)).astype(jnp.bfloat16)
    back = lax.all_to_all(
        result.reshape(device_count, half_cap, width), both, split_axis=0, concat_axis=0, tiled=True
    )
    expert_out = back.reshape(slots_total, width)
    mix_hi = mixing.astype(jnp.bfloat16)
    rest = mixing - mix_hi.astype(jnp.float32)
    mix_mid = rest.astype(jnp.bfloat16)
    mix_lo = (rest - mix_mid.astype(jnp.float32)).astype(jnp.bfloat16)
    mixed = jnp.dot(
        jnp.concatenate([mix_hi, mix_mid, mix_lo], axis=0), expert_out, preferred_element_type=jnp.float32
    ).reshape(3, token_count, width)
    moe = mixed[0] + mixed[1] + mixed[2]
    return (hidden + moe).astype(jnp.bfloat16)


def solution(mesh):
    return jax.shard_map(
        shards,
        mesh=mesh,
        in_specs=(
            P("ctx", "kvh"),
            P("ctx", "kvh"),
            P("ctx", "kvh"),
            P("kvh", None),
            P(("ctx", "kvh"), None),
            P(),
            P(None, ("ctx", "kvh")),
            P(None, ("ctx", "kvh")),
            P(("ctx", "kvh"), None),
            P(("ctx", "kvh"), None),
            P(("ctx", "kvh"), None),
        ),
        out_specs=P(("ctx", "kvh"), None),
        check_vma=False,
    )
```

```python
import jax
import jax.numpy as jnp
from jax import lax
from jax.experimental import pallas as pl
from jax.experimental.pallas import tpu as pltpu
from jax.sharding import PartitionSpec as P

HEAD = 64
GROUP = 4
TOP = 4
BLK = 512
KEYS = 1024
LOW = -1e30
LOG2E = 1.4426950408889634


def flash_kernel(ctx_size, q_ref, kv_ref, o_ref, qs, m_ref, acc):
    me = lax.axis_index("ctx")
    last = 2 * ctx_size - 1
    even = lax.rem(me, 2) == 0
    numbers = (jnp.where(even, me, last - me), jnp.where(even, last - me, me))
    qs[...] = jnp.zeros_like(qs)
    ones = jnp.ones((KEYS, 128), jnp.bfloat16)
    for s in range(2):
        number = numbers[s]
        for h in range(GROUP):
            q = q_ref[s, :, h * HEAD : (h + 1) * HEAD].astype(jnp.float32) * (0.125 * LOG2E)
            hi = q.astype(jnp.bfloat16)
            lo = (q - hi.astype(jnp.float32)).astype(jnp.bfloat16)
            qs[h, :, 0:HEAD] = hi
            qs[h, :, 128 : 128 + HEAD] = lo
        m_ref[...] = jnp.full_like(m_ref, LOW)
        acc[...] = jnp.zeros_like(acc)

        def fold(start, masked, number=number):
            kv = kv_ref[pl.ds(pl.multiple_of(start, BLK), KEYS), :]
            rhs_k = jnp.concatenate([kv, kv], axis=1)
            rhs_v = jnp.concatenate([kv, ones], axis=1)
            if masked:
                row = number * BLK + lax.broadcasted_iota(jnp.int32, (BLK, KEYS), 0)
                col = start + lax.broadcasted_iota(jnp.int32, (BLK, KEYS), 1)
                allowed = row >= col
            for h in range(GROUP):
                sc = lax.dot_general(
                    qs[h], rhs_k, (((1,), (1,)), ((), ())), preferred_element_type=jnp.float32
                )
                if masked:
                    sc = jnp.where(allowed, sc, LOW)
                m_old = m_ref[h]
                m_new = jnp.maximum(m_old, jnp.max(sc, axis=1, keepdims=True))
                alpha = jnp.exp2(m_old - m_new)
                p = jnp.exp2(sc - m_new[:, :1]).astype(jnp.bfloat16)
                pv = jnp.dot(p, rhs_v, preferred_element_type=jnp.float32)
                acc[h] = acc[h] * jnp.concatenate([alpha, alpha], axis=1) + pv
                m_ref[h] = m_new

        half = number // 2

        def body(j, carry, fold=fold):
            fold(j * KEYS, False)
            return carry

        lax.fori_loop(0, half, body, 0)
        fold(half * KEYS, True)
        parts = []
        for h in range(GROUP):
            a = acc[h]
            parts.append(a[:, HEAD : 2 * HEAD] / a[:, 128 : 128 + HEAD])
        o_ref[s] = jnp.concatenate(parts, axis=1).astype(jnp.bfloat16)


def flash(q2, kv_all, ctx_size):
    return pl.pallas_call(
        lambda *refs: flash_kernel(ctx_size, *refs),
        out_shape=jax.ShapeDtypeStruct(q2.shape, jnp.bfloat16),
        in_specs=[pl.BlockSpec(memory_space=pltpu.VMEM)] * 2,
        out_specs=pl.BlockSpec(memory_space=pltpu.VMEM),
        scratch_shapes=[
            pltpu.VMEM((GROUP, BLK, 256), jnp.bfloat16),
            pltpu.VMEM((GROUP, BLK, 128), jnp.float32),
            pltpu.VMEM((GROUP, BLK, 256), jnp.float32),
        ],
        compiler_params=pltpu.CompilerParams(vmem_limit_bytes=48 << 20),
        cost_estimate=pl.CostEstimate(
            flops=80_000_000_000, bytes_accessed=6_000_000, transcendentals=40_000_000
        ),
        name="flash",
    )(q2, kv_all)


def shards(
    query_rows,
    key_rows,
    value_rows,
    out_weight,
    residual,
    norm_gain,
    gate_weight,
    up_weight,
    down_weight,
    expert_ids,
    route_weights,
):
    nc, nk = lax.axis_size("ctx"), lax.axis_size("kvh")
    both = ("ctx", "kvh")
    rows = query_rows.shape[0]
    token_count, width = residual.shape

    swap, cross = [], []
    for zy in range(nc // 2):
        for core in range(2):
            for x in range(nk // 2):
                for y in range(2):
                    here = (zy * 2 + core) * nk + x * 2 + y
                    there = (zy * 2 + y) * nk + x * 2 + core
                    if core != y:
                        swap.append((here, there))
                    cross.append((here, (zy * 2 + 1 - core) * nk + x * 2 + y))
    swapped = (lax.axis_index("ctx") + lax.axis_index("kvh")) % 2 == 1
    mine = [
        jnp.where(swapped, lax.ppermute(w, both, swap), w)
        for w in (gate_weight, up_weight, down_weight)
    ]
    other = [lax.ppermute(w, both, cross) for w in mine]

    kv_all = lax.all_gather(jnp.concatenate([key_rows, value_rows], axis=1), "ctx", axis=0, tiled=True)
    even = [(j, 2 * j if 2 * j < nc else 2 * nc - 1 - 2 * j) for j in range(nc)]
    odd = [(j, 2 * j + 1 if 2 * j + 1 < nc else 2 * nc - 2 - 2 * j) for j in range(nc)]
    q_even = lax.ppermute(query_rows[: rows // 2], "ctx", even)
    q_odd = lax.ppermute(query_rows[rows // 2 :], "ctx", odd)
    attended2 = flash(jnp.stack([q_even, q_odd]), kv_all, nc)
    a_even = lax.ppermute(attended2[0], "ctx", [(b, a) for a, b in even])
    a_odd = lax.ppermute(attended2[1], "ctx", [(b, a) for a, b in odd])
    attended = jnp.concatenate([a_even, a_odd], axis=0)
    along_x = [[y + 2 * x for x in range(nk // 2)] for y in range(2)]
    along_y = [[2 * x, 2 * x + 1] for x in range(nk // 2)]
    weight_all = lax.all_gather(out_weight, "kvh", axis=0, tiled=True, axis_index_groups=along_x)
    heads = lax.all_to_all(
        attended, "kvh", split_axis=0, concat_axis=1, tiled=True, axis_index_groups=along_x
    )
    part = jnp.dot(heads, weight_all, preferred_element_type=jnp.float32).astype(jnp.bfloat16)
    pair = lax.all_to_all(
        part.reshape(2, token_count, width), "kvh", split_axis=0, concat_axis=0, tiled=True, axis_index_groups=along_y
    ).astype(jnp.float32)
    projected = pair[0] + pair[1]
    hidden = residual.astype(jnp.float32) + projected
    normed = (
        hidden * lax.rsqrt(jnp.mean(hidden * hidden, axis=-1, keepdims=True) + 1e-05) * norm_gain
    ).astype(jnp.bfloat16)

    device_count = nc * nk
    expert_count = device_count // 2
    capacity = 2 * max(1, 5 * token_count * TOP // (8 * expert_count))
    half_cap = capacity // 2
    slots_total = expert_count * capacity
    flat_ids = expert_ids.reshape(-1)
    onehot = (flat_ids[:, None] == jnp.arange(expert_count, dtype=jnp.int32)[None, :]).astype(
        jnp.int32
    )
    before = jnp.cumsum(onehot, axis=0) - onehot
    slot = jnp.sum(before * onehot, axis=1)
    per_zy = nk
    zy, c, x = flat_ids // per_zy, (flat_ids // (nk // 2)) % 2, flat_ids % (nk // 2)
    dest = (zy * 2 + slot // half_cap) * nk + x * 2 + c
    target = (dest * half_cap + slot % half_cap).reshape(token_count, TOP)
    slot_iota = jnp.arange(slots_total, dtype=jnp.int32)
    matches = slot_iota[None, None, :] == target[:, :, None]
    placing = jnp.any(matches, axis=1).astype(jnp.bfloat16)
    mixing = jnp.sum(jnp.where(matches, route_weights[:, :, None], 0.0), axis=1)
    outgoing = jnp.einsum("ts,td->sd", placing, normed, preferred_element_type=jnp.float32).astype(
        jnp.bfloat16
    )
    outgoing = outgoing.reshape(device_count, half_cap, width)
    items = lax.all_to_all(outgoing, both, split_axis=0, concat_axis=0, tiled=True)
    flat = items.reshape(slots_total, width)

    def half_expert(gate_w, up_w, down_w):
        gate = jnp.dot(flat, gate_w, preferred_element_type=jnp.float32)
        up = jnp.dot(flat, up_w, preferred_element_type=jnp.float32)
        act = ((up + 1.0) * gate * jax.nn.sigmoid(1.702 * gate)).astype(jnp.bfloat16)
        return jnp.dot(act, down_w, preferred_element_type=jnp.float32)

    result = (half_expert(*mine) + half_expert(*other)).astype(jnp.bfloat16)
    back = lax.all_to_all(
        result.reshape(device_count, half_cap, width), both, split_axis=0, concat_axis=0, tiled=True
    )
    expert_out = back.reshape(slots_total, width)
    mix_hi = mixing.astype(jnp.bfloat16)
    rest = mixing - mix_hi.astype(jnp.float32)
    mix_mid = rest.astype(jnp.bfloat16)
    mix_lo = (rest - mix_mid.astype(jnp.float32)).astype(jnp.bfloat16)
    mixed = jnp.dot(
        jnp.concatenate([mix_hi, mix_mid, mix_lo], axis=0), expert_out, preferred_element_type=jnp.float32
    ).reshape(3, token_count, width)
    moe = mixed[0] + mixed[1] + mixed[2]
    return (hidden + moe).astype(jnp.bfloat16)


def solution(mesh):
    return jax.shard_map(
        shards,
        mesh=mesh,
        in_specs=(
            P("ctx", "kvh"),
            P("ctx", "kvh"),
            P("ctx", "kvh"),
            P("kvh", None),
            P(("ctx", "kvh"), None),
            P(),
            P(None, ("ctx", "kvh")),
            P(None, ("ctx", "kvh")),
            P(("ctx", "kvh"), None),
            P(("ctx", "kvh"), None),
            P(("ctx", "kvh"), None),
        ),
        out_specs=P(("ctx", "kvh"), None),
        check_vma=False,
    )
```
